32 devices in a mesh: expert: 8 (over z, x), dp: 4 (over y, core).
Axes of the slice: x: 2, y: 2, z: 4, core: 2. Of those that a mesh axis runs over, the one named last changes fastest.
Arguments:
- tokens: bfloat16 [1024, 4096], P('expert', 'dp'), may hold values from -6 to 6
- out_grad: bfloat16 [1024, 4096], P('expert', 'dp'), may hold values from -6 to 6
- routes: int32 [1024, 4], P('expert'), may hold values from 0 to 7, all different within a row; in each aligned block of 128 rows (0 to 127, 128 to 255, ...) at most 72 rows name the same one
- gate_weights: float32 [1024, 4], P('expert'), may hold values from 0.05 to 0.5
- previous_home: int32 [8], replicated, may hold values from 0 to 7, each once
- next_home: int32 [8], replicated, may hold values from 0 to 7, each once
- w_in: bfloat16 [8, 2, 4096, 1024], P('expert', None, None, 'dp'), may hold values from -0.09375 to 0.09375
- w_out: bfloat16 [8, 1024, 4096], P('expert', 'dp'), may hold values from -0.1875 to 0.1875
- first_moment: float32 [8, 1024, 4096], P('expert', 'dp'), may hold values from -12 to 12
- second_moment: float32 [8, 1024, 4096], P('expert', 'dp'), may hold values from 1 to 30
Outputs:
- token_grad: bfloat16 [1024, 4096], P('expert', 'dp')
- new_first: float32 [8, 1024, 4096], P('expert', 'dp')
- new_second: float32 [8, 1024, 4096], P('expert', 'dp')
- adam_step: bfloat16 [8, 1024, 4096], P('expert', 'dp')
The draws below stay inside these ranges and needn't reach their ends.
Inputs may be any that keep to these rules, and one draw needn't show every extreme that they name: `routes`: in each device's block of 128 tokens at most 72 pairs name the same expert, and some block reaches 72. `previous_home`: each expert appears once. `next_home`: each expert appears once.
All inputs are finite; a program needn't handle non-finite values.
Results may differ from the reference program's by a relative error of at most 0.0064.
Values may be sent and summed in bfloat16 or wider, within the bound.
No kernel may reach another device: no remote copies, remote signals or barrier semaphores. Data moves between devices by JAX's collectives and lax.ppermute only.
A program may use at most 128 MiB of HBM per device.

```python
import math
import jax
import jax.numpy as jnp
import numpy as np
from jax import lax

D = 4096
FF = 1024
TOP = 4
TOK_DEV = 128
EXPERTS = 8
HID = 256
CAP = 72
TOKENS = 1024
N_EXPERT = 8
N_DP = 4


def level_of(stream_key, shape, pieces, least, largest):
    def one(dim, shards_of):
        heights = jax.random.uniform(jax.random.fold_in(jax.random.fold_in(stream_key, 6), dim), (shards_of,), jnp.float32, least / len(pieces), largest / len(pieces))
        return jnp.repeat(jnp.exp(heights), shape[dim] // shards_of).reshape((-1,) + (1,) * (len(shape) - dim - 1))

    loudness = one(*pieces[0])
    for cut in pieces[1:]:
        loudness = loudness * one(*cut)
    return loudness


def deal_out(own_key, own, number, rows, count, top, limit, slope):
    sequence = jax.random.permutation(own_key, count)
    heavy_load, ordinary = portions_of(count, rows * top, limit, slope, True), portions_of(count, rows * top, limit, slope, False)
    places = jnp.arange(count)

    def named(tallies, offset_by):
        used = int((tallies > 0).sum())
        fixed = max(1, used // 4)
        shifted = fixed + (places - fixed + offset_by * (used - fixed)) % max(1, count - fixed)
        return jnp.zeros((count,), jnp.int32).at[sequence[jnp.where(places < fixed, places, shifted)]].set(jnp.asarray(tallies, jnp.int32))

    tallies = jnp.where(number % 4 == 0, named(heavy_load, number // 4), named(ordinary, number - number // 4 - 1))
    mixed = jax.random.permutation(jax.random.fold_in(own, 3), count)
    source_of, taker = mixed[0:count // 2 * 2:2], mixed[1:count // 2 * 2:2]
    room = jnp.minimum(tallies[source_of] - 1, limit - tallies[taker]) // 2
    room = jnp.where((source_of == sequence[0]) | (taker == sequence[0]) | (tallies[taker] == 0), 0, jnp.maximum(room, 0))
    shifted = jax.random.randint(jax.random.fold_in(own, 4), (count // 2,), 0, 1 << 20) % (room + 1)
    tallies = tallies.at[source_of].add(-shifted).at[taker].add(shifted)
    members = jnp.searchsorted(jnp.cumsum(tallies), jnp.arange(rows * top), side="right").astype(jnp.int32)
    table = members.reshape(top, rows).T
    table = table[jax.random.permutation(jax.random.fold_in(own, 1), rows)]
    offset_by = jax.random.randint(jax.random.fold_in(own, 2), (rows, 1), 0, top)
    return jnp.take_along_axis(table, (jnp.arange(top)[None, :] + offset_by) % top, axis=1)


def portions_of(amount, total, most, lean, full):
    loads = [(1 << 20) // math.isqrt(grade ** lean) + 1 for grade in range(1, amount + 1)]
    largest = most if full else min(most, max(-(-total // amount), total * loads[0] // sum(loads)))
    least = 1 if total - largest >= amount - 1 else 0
    given, spare = [largest] + [least] * (amount - 1), total - largest - least * (amount - 1)
    while spare > 0:
        movable = [i for i in range(1, amount) if given[i] < largest] or [i for i in range(1, amount) if given[i] < most]
        whole, budget = sum([loads[i] for i in movable]), spare
        for i in movable:
            addition = min(most - given[i], max(1, budget * loads[i] // whole), spare)
            given[i] = given[i] + addition
            spare = spare - addition
    return np.array(given)


def normal_values(rng, shape, deviation, reach, pieces=(), held_as=jnp.bfloat16):
    values = jax.random.normal(rng, shape, jnp.float32) * deviation
    if len(pieces) > 0:
        values = level_of(rng, shape, pieces, -0.22, 0.18) * values
    return jnp.clip(values, min=-reach, max=reach).astype(held_as)


def setup_inputs(seed: int = 0) -> dict:
    arg_keys = jax.random.split(jax.random.key(seed), 11)
    tokens = normal_values(arg_keys[0], (TOKENS, D), 1.0, 6.0, ((0, 8), (1, 4)))
    out_grad = normal_values(arg_keys[1], (TOKENS, D), 1.0, 6.0, ((0, 8), (1, 4)))
    routes_keys = jax.random.split(jax.random.fold_in(arg_keys[2], 1), TOKENS // TOK_DEV)
    routes_turns = jax.random.permutation(jax.random.fold_in(arg_keys[2], 3), TOKENS // TOK_DEV)
    routes = jax.vmap(lambda own, number: deal_out(jax.random.fold_in(arg_keys[2], 2), own, number, TOK_DEV, EXPERTS, TOP, CAP, 2))(routes_keys, routes_turns).reshape((TOKENS, TOP))
    gate_weights = jnp.clip(jnp.exp(math.log(0.5) - 2.3025851 * jax.random.uniform(arg_keys[3], (TOKENS, TOP), jnp.float32) ** level_of(arg_keys[3], (TOKENS, TOP), ((0, 8),), -0.2, 0.2)), 0.05, 0.5)
    previous_home = jax.random.permutation(arg_keys[4], EXPERTS).astype(jnp.int32)
    next_home = jax.random.permutation(arg_keys[5], EXPERTS).astype(jnp.int32)
    w_in = normal_values(arg_keys[6], (EXPERTS, 2, D, FF), D ** -0.5, 0.09375, ((0, 8), (3, 4)))
    w_out = normal_values(arg_keys[7], (EXPERTS, FF, D), FF ** -0.5, 0.1875, ((0, 8), (1, 4)))
    first_moment = normal_values(arg_keys[8], (EXPERTS, FF, D), 2.0, 12.0, ((0, 8), (1, 4)), jnp.float32)
    second_moment = jnp.clip(jnp.exp(math.log(30.0) - 3.4011974 * jax.random.uniform(arg_keys[9], (EXPERTS, FF, D), jnp.float32) ** level_of(arg_keys[9], (EXPERTS, FF, D), ((0, 8), (1, 4)), -0.2, 0.2)), 1.0, 30.0)
    return dict(tokens=tokens, out_grad=out_grad, routes=routes, gate_weights=gate_weights, previous_home=previous_home, next_home=next_home, w_in=w_in, w_out=w_out, first_moment=first_moment, second_moment=second_moment)


beta_one = 0.9
beta_two = 0.95
epsilon = 1e-08

def reference(tokens, out_grad, routes, gate_weights, previous_home, next_home, w_in, w_out, first_moment, second_moment):
    pairs = TOKENS * TOP
    onehot = (routes[:, :, None] == jnp.arange(EXPERTS, dtype=jnp.int32)[None, None, :]).astype(jnp.int32)
    onehot = onehot.reshape(N_EXPERT, TOK_DEV * TOP, EXPERTS)
    before = jnp.cumsum(onehot, axis=1) - onehot
    slot_index = lax.optimization_barrier(jnp.sum(before * onehot, axis=2))
    position = jnp.arange(N_EXPERT, dtype=jnp.int32)[:, None] * CAP + slot_index
    pair_table = jnp.full((EXPERTS, N_EXPERT * CAP), pairs, jnp.int32)
    pair_table = pair_table.at[routes.reshape(-1), position.reshape(-1)].set(jnp.arange(pairs, dtype=jnp.int32))
    zero_row = jnp.zeros((1, D), jnp.bfloat16)
    pair_rows = jnp.concatenate([jnp.repeat(tokens, TOP, axis=0), zero_row], axis=0)
    scaled = gate_weights.reshape(-1, 1) * jnp.repeat(out_grad, TOP, axis=0).astype(jnp.float32)
    pair_grads = jnp.concatenate([scaled.astype(jnp.bfloat16), zero_row], axis=0)

    def per_expert(expert):
        chosen = pair_table[expert]
        slot_rows = pair_rows[chosen]
        slot_grads = pair_grads[chosen]
        old_home = previous_home[expert]
        weight_in = w_in[old_home]
        weight_out = w_out[old_home]
        gate_pre = jnp.dot(slot_rows, weight_in[0], preferred_element_type=jnp.float32)
        up_value = jnp.dot(slot_rows, weight_in[1], preferred_element_type=jnp.float32)
        sigmoid_gate = jax.nn.sigmoid(gate_pre)
        silu_gate = gate_pre * sigmoid_gate
        activation = (silu_gate * up_value).astype(jnp.bfloat16)
        weight_grad = jnp.dot(activation.T, slot_grads, preferred_element_type=jnp.float32)
        act_grad = jnp.dot(slot_grads, weight_out.T, preferred_element_type=jnp.float32)
        gate_grad = (act_grad * up_value * sigmoid_gate * (1.0 + gate_pre * (1.0 - sigmoid_gate))).astype(jnp.bfloat16)
        up_grad = (act_grad * silu_gate).astype(jnp.bfloat16)
        summed = jnp.zeros((N_EXPERT * CAP, D), jnp.float32)
        for group_index in range(N_DP):
            lower_edge = group_index * HID
            upper_edge = lower_edge + HID
            partial_value = jnp.dot(gate_grad[:, lower_edge:upper_edge], weight_in[0][:, lower_edge:upper_edge].T, preferred_element_type=jnp.float32)
            partial_value = partial_value + jnp.dot(up_grad[:, lower_edge:upper_edge], weight_in[1][:, lower_edge:upper_edge].T, preferred_element_type=jnp.float32)
            partial_value = lax.optimization_barrier(partial_value.astype(jnp.bfloat16))
            summed = summed + partial_value.astype(jnp.float32)
        moment_one = beta_one * first_moment[old_home] + (1.0 - beta_one) * weight_grad
        moment_two = beta_two * second_moment[old_home] + (1.0 - beta_two) * weight_grad * weight_grad
        step_value = (moment_one / (jnp.sqrt(moment_two) + epsilon)).astype(jnp.bfloat16)
        return (moment_one, moment_two, step_value, summed)
    moment_one, moment_two, step_value, slot_sums = lax.map(per_expert, jnp.arange(EXPERTS, dtype=jnp.int32))
    pair_sum = jnp.zeros((pairs + 1, D), jnp.float32).at[pair_table.reshape(-1)].add(slot_sums.reshape(-1, D))
    token_grad = pair_sum[:pairs].reshape(TOKENS, TOP, D).sum(axis=1).astype(jnp.bfloat16)
    new_first = jnp.zeros_like(moment_one).at[next_home].set(moment_one)
    new_second = jnp.zeros_like(moment_two).at[next_home].set(moment_two)
    adam_step = jnp.zeros_like(step_value).at[next_home].set(step_value)
    return (token_grad, new_first, new_second, adam_step)
```

```python
import jax
import jax.numpy as jnp
from jax import lax
from jax.sharding import PartitionSpec as P

beta_one = 0.9
beta_two = 0.95
epsilon = 1e-08


def swap(value, axis, mask):
    size = lax.axis_size(axis)
    return lax.ppermute(value, axis, [(j, j ^ mask) for j in range(size)])


def gather_parts(value, axis):
    parts = {0: value}
    mask = lax.axis_size(axis) // 2
    while mask:
        parts.update({k ^ mask: swap(v, axis, mask) for k, v in list(parts.items())})
        mask //= 2
    return [parts[k] for k in range(len(parts))]


def scatter_sum(parts, axis):
    parts = dict(enumerate(parts))
    mask = 1
    while len(parts) > 1:
        kept = {}
        for k in [k for k in parts if not k & mask]:
            other = swap(parts[k ^ mask].astype(jnp.bfloat16), axis, mask)
            kept[k] = parts[k].astype(jnp.float32) + other.astype(jnp.float32)
        parts = kept
        mask *= 2
    return parts[0]


def spread(value):
    return lax.all_to_all(value, "expert", split_axis=0, concat_axis=0, tiled=True)


def dot(left, right, dims):
    return lax.dot_general(left, right, (dims, ((), ())), preferred_element_type=jnp.float32)


def per_device(
    tokens,
    out_grad,
    routes,
    gate_weights,
    previous_home,
    next_home,
    w_in,
    w_out,
    first_moment,
    second_moment,
):
    devices = lax.axis_size("expert")
    ways = lax.axis_size("dp")
    half = devices // 2
    tok_count, top_count = routes.shape
    experts = previous_home.shape[0]
    capacity = tok_count * top_count * 9 // (8 * experts)
    slots = devices * capacity
    columns = tokens.shape[1]
    hidden = w_out.shape[1]
    width = w_out.shape[2]
    place = lax.axis_index("expert")
    side = place // half
    lane = lax.axis_index("dp")
    halves = [list(range(half)), list(range(half, devices))]

    homes = jnp.arange(devices, dtype=jnp.int32)
    matched = (next_home[:, None] == homes[None, :]).astype(jnp.int32)
    source = jnp.sum(matched * previous_home[:, None], axis=0)

    def relocate(value):
        rows = value.shape[0] // devices
        pieces = spread(value.reshape(devices, rows, value.shape[1]))
        pieces = jnp.take(pieces, source, axis=0)
        return spread(pieces).reshape(value.shape)

    def across_half(value):
        return lax.all_to_all(
            value, "expert", split_axis=0, concat_axis=0, tiled=True, axis_index_groups=halves
        )

    far_tokens = swap(tokens, "expert", half)
    far_routes = swap(routes, "expert", half)
    far_gates = swap(gate_weights, "expert", half)
    far_grads = swap(out_grad, "expert", half)

    old_first = relocate(first_moment[0].astype(jnp.bfloat16))
    old_second = relocate(second_moment[0].astype(jnp.bfloat16))

    both_routes = jnp.stack([routes, far_routes])
    both_gates = jnp.stack([gate_weights, far_gates])
    both_tokens = jnp.concatenate([tokens, far_tokens], axis=0)
    both_grads = jnp.concatenate([out_grad, far_grads], axis=0)
    block_side = jnp.stack([side, 1 - side]).astype(jnp.float32)
    earlier = jnp.tril(jnp.ones((tok_count, tok_count), jnp.bfloat16), -1)
    own_homes = side * half + jnp.arange(half, dtype=jnp.int32)

    def selection(home_table):
        chosen = (home_table[None, :] == own_homes[:, None]).astype(jnp.int32)
        expert_of = jnp.sum(chosen * jnp.arange(experts, dtype=jnp.int32)[None, :], axis=1)
        hit = both_routes[:, None, :, :] == expert_of[None, :, None, None]
        member = jnp.any(hit, axis=3)
        gate = jnp.sum(jnp.where(hit, both_gates[:, None, :, :], 0.0), axis=3)
        before = dot(member.astype(jnp.bfloat16), earlier, (((2,), (1,))))
        slot = jnp.where(member, before + block_side[:, None, None] * capacity, -1.0)
        slot = jnp.concatenate([slot[0], slot[1]], axis=1)
        gate = jnp.concatenate([gate[0], gate[1]], axis=1)
        numbers = lax.broadcasted_iota(jnp.int32, (half, 2 * capacity, 2 * tok_count), 1)
        picks = numbers == slot.astype(jnp.int32)[:, None, :]
        slot_gate = jnp.sum(jnp.where(picks, gate[:, None, :], 0.0), axis=2)
        picks = picks.astype(jnp.bfloat16).reshape(slots, 2 * tok_count)
        return picks, slot_gate.reshape(slots, 1)

    picks_now, gate_now = selection(previous_home)
    picks_next, gate_next = selection(next_home)

    def send(rows):
        rows = rows.astype(jnp.bfloat16).reshape(half, 2 * capacity, columns)
        return across_half(rows).reshape(slots, columns)

    plain = ((1,), (0,))
    rows_parts = gather_parts(send(dot(picks_now, both_tokens, plain)), "dp")
    grad_parts = gather_parts(send(dot(picks_now, both_grads, plain) * gate_now), "dp")
    next_parts = gather_parts(send(dot(picks_next, both_grads, plain) * gate_next), "dp")

    order = lane ^ jnp.arange(ways, dtype=jnp.int32)
    weight_in = jnp.concatenate([w_in[0, 0], w_in[0, 1]], axis=1).reshape(ways, columns, 2 * hidden)
    weight_out = w_out[0].reshape(hidden, ways, columns)
    weight_in = [lax.dynamic_index_in_dim(weight_in, order[k], 0, False) for k in range(ways)]
    weight_out = [lax.dynamic_index_in_dim(weight_out, order[k], 1, False) for k in range(ways)]

    pre = sum(dot(rows_parts[k], weight_in[k], plain) for k in range(ways))
    gate_pre, up_value = pre[:, :hidden], pre[:, hidden:]
    sigmoid_gate = jax.nn.sigmoid(gate_pre)
    silu_gate = gate_pre * sigmoid_gate
    activation = relocate((silu_gate * up_value).astype(jnp.bfloat16))
    act_grad = sum(dot(grad_parts[k], weight_out[k], ((1,), (1,))) for k in range(ways))
    gate_grad = act_grad * up_value * sigmoid_gate * (1.0 + gate_pre * (1.0 - sigmoid_gate))
    up_grad = act_grad * silu_gate
    both_grad = jnp.concatenate([gate_grad, up_grad], axis=1).astype(jnp.bfloat16)
    pieces = [dot(both_grad, weight_in[k], ((1,), (1,))).astype(jnp.bfloat16) for k in range(ways)]
    summed = scatter_sum(pieces, "dp").astype(jnp.bfloat16)
    returned = across_half(summed.reshape(half, 2 * capacity, columns)).reshape(slots, columns)
    token_sums = dot(picks_now, returned, ((0,), (0,)))
    far_sums = swap(token_sums[tok_count:].astype(jnp.bfloat16), "expert", half)
    token_grad = (token_sums[:tok_count] + far_sums.astype(jnp.float32)).astype(jnp.bfloat16)

    weight_grad = jnp.stack([dot(activation, part, ((0,), (0,))) for part in next_parts])
    weight_grad = jnp.take(weight_grad, order, axis=0)
    weight_grad = jnp.swapaxes(weight_grad, 0, 1).reshape(hidden, width)
    new_first = beta_one * old_first.astype(jnp.float32) + (1.0 - beta_one) * weight_grad
    new_second = (
        beta_two * old_second.astype(jnp.float32) + (1.0 - beta_two) * weight_grad * weight_grad
    )
    adam_step = (new_first / (jnp.sqrt(new_second) + epsilon)).astype(jnp.bfloat16)
    return (token_grad, new_first[None], new_second[None], adam_step[None])


def solution(mesh):
    return jax.shard_map(
        per_device,
        mesh=mesh,
        in_specs=(
            P("expert", "dp"),
            P("expert", "dp"),
            P("expert", None),
            P("expert", None),
            P(),
            P(),
            P("expert", None, None, "dp"),
            P("expert", "dp", None),
            P("expert", "dp", None),
            P("expert", "dp", None),
        ),
        out_specs=(
            P("expert", "dp"),
            P("expert", "dp", None),
            P("expert", "dp", None),
            P("expert", "dp", None),
        ),
        check_vma=False,
    )
```

```python
import jax
import jax.numpy as jnp
from jax import lax
from jax.experimental import pallas as pl
from jax.experimental.pallas import tpu as pltpu
from jax.sharding import PartitionSpec as P


beta_one = 0.9
beta_two = 0.95
epsilon = 1e-08


def swap(value, axis, mask):
    size = lax.axis_size(axis)
    return lax.ppermute(value, axis, [(j, j ^ mask) for j in range(size)])


def gather_parts(value, axis):
    parts = {0: value}
    mask = lax.axis_size(axis) // 2
    while mask:
        parts.update({k ^ mask: swap(v, axis, mask) for k, v in list(parts.items())})
        mask //= 2
    return [parts[k] for k in range(len(parts))]


def scatter_sum(parts, axis):
    parts = dict(enumerate(parts))
    mask = 1
    while len(parts) > 1:
        kept = {}
        for k in [k for k in parts if not k & mask]:
            other = swap(parts[k ^ mask].astype(jnp.bfloat16), axis, mask)
            kept[k] = parts[k].astype(jnp.float32) + other.astype(jnp.float32)
        parts = kept
        mask *= 2
    return parts[0]


def finish_body(lane_ref, grad_ref, first_ref, second_ref, out_first, out_second, out_step):
    weight_grad = grad_ref[0]
    new_first = beta_one * first_ref[...].astype(jnp.float32) + (1.0 - beta_one) * weight_grad
    scaled = (1.0 - beta_two) * weight_grad * weight_grad
    new_second = beta_two * second_ref[...].astype(jnp.float32) + scaled
    out_first[...] = new_first
    out_second[...] = new_second
    out_step[...] = (new_first / (jnp.sqrt(new_second) + epsilon)).astype(jnp.bfloat16)


def finish(lane, weight_grad, first, second):
    ways, hidden, columns = weight_grad.shape
    rows = max(hidden // 4, 16)
    wide = pl.BlockSpec((rows, columns), lambda k, i, lane: (i, lane[0] ^ k))
    shape = (hidden, ways * columns)
    return pl.pallas_call(
        finish_body,
        out_shape=(
            jax.ShapeDtypeStruct(shape, jnp.float32),
            jax.ShapeDtypeStruct(shape, jnp.float32),
            jax.ShapeDtypeStruct(shape, jnp.bfloat16),
        ),
        grid_spec=pltpu.PrefetchScalarGridSpec(
            num_scalar_prefetch=1,
            grid=(ways, hidden // rows),
            in_specs=[
                pl.BlockSpec((1, rows, columns), lambda k, i, lane: (k, i, 0)),
                wide,
                wide,
            ],
            out_specs=(wide, wide, wide),
        ),
        name="finish",
    )(lane.reshape(1), weight_grad, first, second)


def spread(value):
    return lax.all_to_all(value, "expert", split_axis=0, concat_axis=0, tiled=True)


def dot(left, right, dims):
    return lax.dot_general(left, right, (dims, ((), ())), preferred_element_type=jnp.float32)


def per_device(
    tokens,
    out_grad,
    routes,
    gate_weights,
    previous_home,
    next_home,
    w_in,
    w_out,
    first_moment,
    second_moment,
):
    devices = lax.axis_size("expert")
    ways = lax.axis_size("dp")
    half = devices // 2
    tok_count, top_count = routes.shape
    experts = previous_home.shape[0]
    capacity = tok_count * top_count * 9 // (8 * experts)
    slots = devices * capacity
    columns = tokens.shape[1]
    hidden = w_out.shape[1]
    place = lax.axis_index("expert")
    side = place // half
    lane = lax.axis_index("dp")
    spot = (place % half) ^ jnp.arange(half, dtype=jnp.int32)

    homes = jnp.arange(devices, dtype=jnp.int32)
    matched = (next_home[:, None] == homes[None, :]).astype(jnp.int32)
    source = jnp.sum(matched * previous_home[:, None], axis=0)

    def relocate(value):
        rows = value.shape[0] // devices
        pieces = spread(value.reshape(devices, rows, value.shape[1]))
        pieces = jnp.take(pieces, source, axis=0)
        return spread(pieces).reshape(value.shape)

    def across_half(blocks):
        moved = [blocks[r] if r == 0 else swap(blocks[r], "expert", r) for r in range(half)]
        return jnp.concatenate(moved, axis=0)

    far_tokens = swap(tokens, "expert", half)
    far_routes = swap(routes, "expert", half)
    far_gates = swap(gate_weights, "expert", half)
    far_grads = swap(out_grad, "expert", half)

    old_first = relocate(first_moment[0].astype(jnp.bfloat16))
    old_second = relocate(second_moment[0].astype(jnp.bfloat16))

    both_routes = jnp.stack([routes, far_routes])
    both_gates = jnp.stack([gate_weights, far_gates])
    both_tokens = jnp.concatenate([tokens, far_tokens], axis=0)
    both_grads = jnp.concatenate([out_grad, far_grads], axis=0)
    block_side = jnp.stack([side, 1 - side]).astype(jnp.float32)
    earlier = jnp.tril(jnp.ones((tok_count, tok_count), jnp.bfloat16), -1)
    own_homes = place ^ jnp.arange(half, dtype=jnp.int32)

    def selection(home_table):
        chosen = (home_table[None, :] == own_homes[:, None]).astype(jnp.int32)
        expert_of = jnp.sum(chosen * jnp.arange(experts, dtype=jnp.int32)[None, :], axis=1)
        hit = both_routes[:, None, :, :] == expert_of[None, :, None, None]
        member = jnp.any(hit, axis=3)
        gate = jnp.sum(jnp.where(hit, both_gates[:, None, :, :], 0.0), axis=3)
        before = dot(member.astype(jnp.bfloat16), earlier, (((2,), (1,))))
        slot = jnp.where(member, before + block_side[:, None, None] * capacity, -1.0)
        slot = jnp.concatenate([slot[0], slot[1]], axis=1)
        gate = jnp.concatenate([gate[0], gate[1]], axis=1)
        numbers = lax.broadcasted_iota(jnp.int32, (half, 2 * capacity, 2 * tok_count), 1)
        picks = numbers == slot.astype(jnp.int32)[:, None, :]
        slot_gate = jnp.sum(jnp.where(picks, gate[:, None, :], 0.0), axis=2)
        picks = picks.astype(jnp.bfloat16).reshape(slots, 2 * tok_count)
        return picks, slot_gate.reshape(slots, 1)

    picks_now, gate_now = selection(previous_home)
    picks_next, gate_next = selection(next_home)

    def send(rows):
        rows = rows.astype(jnp.bfloat16).reshape(half, 2 * capacity, columns)
        return across_half(rows)

    plain = ((1,), (0,))

    def deliver(rows):
        rows = send(rows)
        return gather_parts(rows, "dp")

    rows_parts = deliver(dot(picks_now, both_tokens, plain))
    grad_parts = deliver(dot(picks_now, both_grads, plain) * gate_now)
    next_parts = deliver(dot(picks_next, both_grads, plain) * gate_next)

    order = lane ^ jnp.arange(ways, dtype=jnp.int32)
    weight_in = jnp.concatenate([w_in[0, 0], w_in[0, 1]], axis=1).reshape(ways, columns, 2 * hidden)
    weight_out = w_out[0].reshape(hidden, ways, columns)
    weight_in = [lax.dynamic_index_in_dim(weight_in, order[k], 0, False) for k in range(ways)]
    weight_out = [lax.dynamic_index_in_dim(weight_out, order[k], 1, False) for k in range(ways)]

    pre = sum(dot(rows_parts[k], weight_in[k], plain) for k in range(ways))
    gate_pre, up_value = pre[:, :hidden], pre[:, hidden:]
    sigmoid_gate = jax.nn.sigmoid(gate_pre)
    silu_gate = gate_pre * sigmoid_gate
    activation = (silu_gate * up_value).astype(jnp.bfloat16).reshape(half, 2 * capacity, hidden)
    activation = jnp.take(activation, spot, axis=0).reshape(slots, hidden)
    activation = relocate(activation)
    activation = jnp.take(activation.reshape(half, 2 * capacity, hidden), spot, axis=0)
    activation = activation.reshape(slots, hidden)
    act_grad = sum(dot(grad_parts[k], weight_out[k], ((1,), (1,))) for k in range(ways))
    gate_grad = act_grad * up_value * sigmoid_gate * (1.0 + gate_pre * (1.0 - sigmoid_gate))
    up_grad = act_grad * silu_gate
    both_grad = jnp.concatenate([gate_grad, up_grad], axis=1).astype(jnp.bfloat16)
    pieces = [dot(both_grad, weight_in[k], ((1,), (1,))).astype(jnp.bfloat16) for k in range(ways)]
    summed = scatter_sum(pieces, "dp").astype(jnp.bfloat16)
    returned = across_half(summed.reshape(half, 2 * capacity, columns))
    token_sums = dot(picks_now, returned, ((0,), (0,)))
    far_sums = swap(token_sums[tok_count:].astype(jnp.bfloat16), "expert", half)
    token_grad = (token_sums[:tok_count] + far_sums.astype(jnp.float32)).astype(jnp.bfloat16)

    weight_grad = jnp.stack([dot(activation, part, ((0,), (0,))) for part in next_parts])
    new_first, new_second, adam_step = finish(lane, weight_grad, old_first, old_second)
    return (token_grad, new_first[None], new_second[None], adam_step[None])


def solution(mesh):
    return jax.shard_map(
        per_device,
        mesh=mesh,
        in_specs=(
            P("expert", "dp"),
            P("expert", "dp"),
            P("expert", None),
            P("expert", None),
            P(),
            P(),
            P("expert", None, None, "dp"),
            P("expert", "dp", None),
            P("expert", "dp", None),
            P("expert", "dp", None),
        ),
        out_specs=(
            P("expert", "dp"),
            P("expert", "dp", None),
            P("expert", "dp", None),
            P("expert", "dp", None),
        ),
        check_vma=False,
    )
```

```python
import jax
import jax.numpy as jnp
from jax import lax
from jax.experimental import pallas as pl
from jax.experimental.pallas import tpu as pltpu
from jax.sharding import PartitionSpec as P


beta_one = 0.9
beta_two = 0.95
epsilon = 1e-08


def swap(value, axis, mask):
    size = lax.axis_size(axis)
    return lax.ppermute(value, axis, [(j, j ^ mask) for j in range(size)])


def gather_parts(value, axis):
    parts = {0: value}
    mask = lax.axis_size(axis) // 2
    while mask:
        parts.update({k ^ mask: swap(v, axis, mask) for k, v in list(parts.items())})
        mask //= 2
    return [parts[k] for k in range(len(parts))]


def scatter_sum(parts, axis):
    parts = dict(enumerate(parts))
    mask = 1
    while len(parts) > 1:
        kept = {}
        for k in [k for k in parts if not k & mask]:
            other = swap(parts[k ^ mask].astype(jnp.bfloat16), axis, mask)
            kept[k] = parts[k].astype(jnp.float32) + other.astype(jnp.float32)
        parts = kept
        mask *= 2
    return parts[0].astype(jnp.bfloat16)


def first_body(lane_ref, grad_ref, first_ref, out_first):
    out_first[...] = (
        beta_one * first_ref[...].astype(jnp.float32) + (1.0 - beta_one) * grad_ref[0]
    )


def second_body(lane_ref, grad_ref, first_ref, second_ref, out_second, out_step):
    weight_grad = grad_ref[0]
    new_first = beta_one * first_ref[...].astype(jnp.float32) + (1.0 - beta_one) * weight_grad
    scaled = (1.0 - beta_two) * weight_grad * weight_grad
    new_second = beta_two * second_ref[...].astype(jnp.float32) + scaled
    out_second[...] = new_second
    out_step[...] = (new_first / (jnp.sqrt(new_second) + epsilon)).astype(jnp.bfloat16)


def finish(body, lane, weight_grad, moments, kinds):
    ways, hidden, columns = weight_grad.shape
    rows = max(hidden // 2, 16)
    wide = pl.BlockSpec((rows, columns), lambda k, i, lane: (i, lane[0] ^ k))
    return pl.pallas_call(
        body,
        out_shape=tuple(jax.ShapeDtypeStruct((hidden, ways * columns), kind) for kind in kinds),
        grid_spec=pltpu.PrefetchScalarGridSpec(
            num_scalar_prefetch=1,
            grid=(ways, hidden // rows),
            in_specs=[pl.BlockSpec((1, rows, columns), lambda k, i, lane: (k, i, 0))]
            + [wide] * len(moments),
            out_specs=tuple(wide for _ in kinds),
        ),
    )(lane.reshape(1), weight_grad, *moments)


def spread(value):
    return lax.all_to_all(value, "expert", split_axis=0, concat_axis=0, tiled=True)


def dot(left, right, dims):
    return lax.dot_general(left, right, (dims, ((), ())), preferred_element_type=jnp.float32)


PLAIN = ((1,), (0,))
COLUMNS = ((1,), (1,))
ROWS = ((0,), (0,))


def per_device(
    tokens,
    out_grad,
    routes,
    gate_weights,
    previous_home,
    next_home,
    w_in,
    w_out,
    first_moment,
    second_moment,
):
    devices = lax.axis_size("expert")
    ways = lax.axis_size("dp")
    half = devices // 2
    tok_count, top_count = routes.shape
    experts = previous_home.shape[0]
    capacity = tok_count * top_count * 9 // (8 * experts)
    columns = tokens.shape[1]
    hidden = w_out.shape[1]
    place = lax.axis_index("expert")
    lane = lax.axis_index("dp")

    homes = jnp.arange(devices, dtype=jnp.int32)
    matched = (next_home[:, None] == homes[None, :]).astype(jnp.int32)
    source = jnp.sum(matched * previous_home[:, None], axis=0)

    def pick(stack, index):
        return jnp.take(stack, index, axis=0, mode="clip")

    def relocate(value):
        rows = value.shape[0] // devices
        pieces = spread(value.reshape(devices, rows, value.shape[1]))
        pieces = pick(pieces, source)
        return spread(pieces).reshape(value.shape)

    def by_mask(blocks):
        return [swap(b, "expert", k) if k else b for k, b in enumerate(blocks)]

    def cross(value):
        return swap(value, "expert", half)

    far_routes = cross(routes)
    far_gates = cross(gate_weights)
    far_tokens = cross(tokens)
    far_grads = cross(out_grad)

    old_first = relocate(first_moment[0].astype(jnp.bfloat16))
    old_second = relocate(second_moment[0].astype(jnp.bfloat16))

    earlier = jnp.tril(jnp.ones((tok_count, tok_count), jnp.bfloat16), -1)
    near_homes = place ^ jnp.arange(half, dtype=jnp.int32)

    def selection(home_table, routes, gates):
        chosen = (home_table[None, :] == near_homes[:, None]).astype(jnp.int32)
        expert_of = jnp.sum(chosen * jnp.arange(experts, dtype=jnp.int32)[None, :], axis=1)
        hit = routes[None, :, :] == expert_of[:, None, None]
        member = jnp.any(hit, axis=2)
        gate = jnp.sum(jnp.where(hit, gates[None, :, :], 0.0), axis=2)
        before = dot(member.astype(jnp.bfloat16), earlier, COLUMNS)
        slot = jnp.where(member, before, -1.0).astype(jnp.int32)
        numbers = lax.broadcasted_iota(jnp.int32, (half, capacity, tok_count), 1)
        picks = numbers == slot[:, None, :]
        slot_gate = jnp.sum(jnp.where(picks, gate[:, None, :], 0.0), axis=2)
        picks = picks.astype(jnp.bfloat16).reshape(half * capacity, tok_count)
        return picks, slot_gate.reshape(half * capacity, 1)

    def blocks_of(rows):
        rows = rows.astype(jnp.bfloat16).reshape(half, capacity, columns)
        return [rows[r] for r in range(half)]

    def gather(blocks):
        rows = jnp.concatenate(blocks, axis=0)
        return gather_parts(rows, "dp")

    order = lane ^ jnp.arange(ways, dtype=jnp.int32)
    weight_in = jnp.concatenate([w_in[0, 0], w_in[0, 1]], axis=1).reshape(ways, columns, 2 * hidden)
    weight_out = w_out[0].reshape(hidden, ways, columns)
    weight_in = [lax.dynamic_index_in_dim(weight_in, order[k], 0, False) for k in range(ways)]
    weight_out = [lax.dynamic_index_in_dim(weight_out, order[k], 1, False) for k in range(ways)]

    sides = (
        (tokens, out_grad, routes, gate_weights), (far_tokens, far_grads, far_routes, far_gates)
    )
    activations = []
    next_blocks = []
    sums = []
    for side_tokens, side_grads, side_routes, side_gates in sides:
        picks, slot_gate = selection(previous_home, side_routes, side_gates)
        next_picks, next_gate = selection(next_home, side_routes, side_gates)
        rows = by_mask(blocks_of(dot(picks, side_tokens, PLAIN)))
        grads = by_mask(blocks_of(dot(picks, side_grads, PLAIN) * slot_gate))
        rows = gather(rows)
        grads = gather(grads)
        next_rows = blocks_of(dot(next_picks, side_grads, PLAIN) * next_gate)
        next_blocks += by_mask(next_rows)
        pre = sum(dot(rows[k], weight_in[k], PLAIN) for k in range(ways))
        gate_pre, up_value = pre[:, :hidden], pre[:, hidden:]
        sigmoid_gate = jax.nn.sigmoid(gate_pre)
        silu_gate = gate_pre * sigmoid_gate
        activation = (silu_gate * up_value).astype(jnp.bfloat16)
        activations.append(activation.reshape(half, capacity, hidden))
        act_grad = sum(dot(grads[k], weight_out[k], COLUMNS) for k in range(ways))
        slope = 1.0 + gate_pre * (1.0 - sigmoid_gate)
        gate_grad = act_grad * up_value * sigmoid_gate * slope
        up_grad = act_grad * silu_gate
        both_grad = jnp.concatenate([gate_grad, up_grad], axis=1).astype(jnp.bfloat16)
        pieces = [dot(both_grad, weight_in[k], COLUMNS).astype(jnp.bfloat16) for k in range(ways)]
        summed = scatter_sum(pieces, "dp")
        returned = by_mask(blocks_of(summed))
        sums.append(dot(picks, jnp.concatenate(returned, axis=0), ROWS))
    far_sums = cross(sums[1].astype(jnp.bfloat16))
    token_grad = (sums[0] + far_sums.astype(jnp.float32)).astype(jnp.bfloat16)

    activation = jnp.concatenate(activations, axis=0)
    held = jnp.stack(by_mask([activation[k] for k in range(devices)]))
    held = pick(held, place ^ source[place ^ homes])
    activation = by_mask([held[k] for k in range(devices)])
    activation = jnp.concatenate(activation, axis=0)
    next_parts = gather(next_blocks)
    weight_grad = jnp.stack([dot(activation, part, ROWS) for part in next_parts])
    single, pair = (jnp.float32,), (jnp.float32, jnp.bfloat16)
    (new_first,) = finish(first_body, lane, weight_grad, (old_first,), single)
    new_second, adam_step = finish(second_body, lane, weight_grad, (old_first, old_second), pair)
    return (token_grad, new_first[None], new_second[None], adam_step[None])


def solution(mesh):
    return jax.shard_map(
        per_device,
        mesh=mesh,
        in_specs=(
            P("expert", "dp"),
            P("expert", "dp"),
            P("expert", None),
            P("expert", None),
            P(),
            P(),
            P("expert", None, None, "dp"),
            P("expert", "dp", None),
            P("expert", "dp", None),
            P("expert", "dp", None),
        ),
        out_specs=(
            P("expert", "dp"),
            P("expert", "dp", None),
            P("expert", "dp", None),
            P("expert", "dp", None),
        ),
        check_vma=False,
    )
```

```python
import jax
import jax.numpy as jnp
from jax import lax
from jax.experimental import pallas as pl
from jax.experimental.pallas import tpu as pltpu
from jax.sharding import PartitionSpec as P


beta_one = 0.9
beta_two = 0.95
epsilon = 1e-08


def swap(value, axis, mask):
    size = lax.axis_size(axis)
    return lax.ppermute(value, axis, [(j, j ^ mask) for j in range(size)])


def gather_parts(value, axis):
    parts = {0: value}
    mask = lax.axis_size(axis) // 2
    while mask:
        parts.update({k ^ mask: swap(v, axis, mask) for k, v in list(parts.items())})
        mask //= 2
    return [parts[k] for k in range(len(parts))]


def scatter_sum(parts, axis):
    parts = dict(enumerate(parts))
    mask = 1
    while len(parts) > 1:
        kept = {}
        for k in [k for k in parts if not k & mask]:
            other = swap(parts[k ^ mask].astype(jnp.bfloat16), axis, mask)
            kept[k] = parts[k].astype(jnp.float32) + other.astype(jnp.float32)
        parts = kept
        mask *= 2
    return parts[0]


def finish_body(lane_ref, grad_ref, first_ref, second_ref, *refs):
    out_first, out_second, out_step = refs[-3:]
    weight_grad = grad_ref[0]
    new_first = beta_one * first_ref[...].astype(jnp.float32) + (1.0 - beta_one) * weight_grad
    scaled = (1.0 - beta_two) * weight_grad * weight_grad
    new_second = beta_two * second_ref[...].astype(jnp.float32) + scaled
    out_first[...] = new_first
    out_second[...] = new_second
    out_step[...] = (new_first / (jnp.sqrt(new_second) + epsilon)).astype(jnp.bfloat16)


def finish(part, lane, weight_grad, moments, earlier):
    ways, hidden, columns = weight_grad.shape
    rows = max(hidden // 4, 16)
    few = ways // 2
    out = pl.BlockSpec((rows, columns), lambda d, i, lane: (i, part * few + d))
    kinds = (jnp.float32, jnp.float32, jnp.bfloat16)
    return pl.pallas_call(
        finish_body,
        out_shape=tuple(jax.ShapeDtypeStruct((hidden, ways * columns), kind) for kind in kinds),
        grid_spec=pltpu.PrefetchScalarGridSpec(
            num_scalar_prefetch=1,
            grid=(few, hidden // rows),
            in_specs=[
                pl.BlockSpec(
                    (1, rows, columns), lambda d, i, lane: (lane[0] ^ (part * few + d), i, 0)
                ),
                pl.BlockSpec((rows, columns), lambda d, i, lane: (i, d)),
                pl.BlockSpec((rows, columns), lambda d, i, lane: (i, few + d)),
            ]
            + [pl.BlockSpec(memory_space=pl.ANY)] * len(earlier),
            out_specs=(out, out, out),
        ),
        input_output_aliases={4 + k: k for k in range(len(earlier))},
    )(lane.reshape(1), weight_grad, moments, moments, *earlier)


def spread(value):
    return lax.all_to_all(value, "expert", split_axis=0, concat_axis=0, tiled=True)


def dot(left, right, dims):
    return lax.dot_general(left, right, (dims, ((), ())), preferred_element_type=jnp.float32)


ROWS = ((0,), (0,))
COLUMNS = ((1,), (1,))


def per_device(
    tokens,
    out_grad,
    routes,
    gate_weights,
    previous_home,
    next_home,
    w_in,
    w_out,
    first_moment,
    second_moment,
):
    devices = lax.axis_size("expert")
    ways = lax.axis_size("dp")
    half = devices // 2
    tok_count, top_count = routes.shape
    experts = previous_home.shape[0]
    capacity = tok_count * top_count * 9 // (8 * experts)
    slots = devices * capacity
    columns = tokens.shape[1]
    hidden = w_out.shape[1]
    place = lax.axis_index("expert")
    side = place // half
    lane = lax.axis_index("dp")

    homes = jnp.arange(devices, dtype=jnp.int32)
    matched = (next_home[:, None] == homes[None, :]).astype(jnp.int32)
    source = jnp.sum(matched * previous_home[:, None], axis=0)

    def pick(stack, index):
        return jnp.take(stack, index, axis=0, mode="clip")

    def relocate(value):
        rows = value.shape[0] // devices
        pieces = spread(value.reshape(devices, rows, value.shape[1]))
        pieces = pick(pieces, source)
        return spread(pieces).reshape(value.shape)

    def across_half(blocks):
        return [blocks[r] if r == 0 else swap(blocks[r], "expert", r) for r in range(half)]

    def cross(value):
        return swap(value, "expert", half)

    far_routes = cross(routes)
    far_gates = cross(gate_weights)
    far_tokens = cross(tokens)
    far_grads = cross(out_grad)

    middle = w_out.shape[2] // 2
    packed = []
    for cut in (slice(0, middle), slice(middle, None)):
        pieces = (first_moment[0][:, cut], second_moment[0][:, cut])
        packed.append(jnp.concatenate(pieces, axis=1).astype(jnp.bfloat16))
    old_first = relocate(packed[0])
    old_second = relocate(packed[1])

    both_routes = jnp.stack([routes, far_routes])
    both_gates = jnp.stack([gate_weights, far_gates])
    both_tokens = jnp.concatenate([tokens, far_tokens], axis=0)
    both_grads = jnp.concatenate([out_grad, far_grads], axis=0)
    block_side = jnp.stack([side, 1 - side]).astype(jnp.float32)
    earlier = jnp.tril(jnp.ones((tok_count, tok_count), jnp.bfloat16), -1)
    own_homes = place ^ jnp.arange(half, dtype=jnp.int32)

    def selection(home_table):
        chosen = (home_table[None, :] == own_homes[:, None]).astype(jnp.int32)
        expert_of = jnp.sum(chosen * jnp.arange(experts, dtype=jnp.int32)[None, :], axis=1)
        hit = both_routes[:, None, :, :] == expert_of[None, :, None, None]
        member = jnp.any(hit, axis=3)
        gate = jnp.sum(jnp.where(hit, both_gates[:, None, :, :], 0.0), axis=3)
        before = dot(member.astype(jnp.bfloat16), earlier, (((2,), (1,))))
        slot = jnp.where(member, before + block_side[:, None, None] * capacity, -1.0)
        slot = jnp.concatenate([slot[0], slot[1]], axis=1)
        gate = jnp.concatenate([gate[0], gate[1]], axis=1)
        numbers = lax.broadcasted_iota(jnp.int32, (half, 2 * capacity, 2 * tok_count), 1)
        picks = numbers == slot.astype(jnp.int32)[:, None, :]
        slot_gate = jnp.sum(jnp.where(picks, gate[:, None, :], 0.0), axis=2)
        picks = picks.astype(jnp.bfloat16).reshape(slots, 2 * tok_count)
        return picks, slot_gate.reshape(slots, 1)

    picks_now, gate_now = selection(previous_home)
    picks_next, gate_next = selection(next_home)

    def send(rows):
        rows = rows.astype(jnp.bfloat16).reshape(half, 2 * capacity, columns)
        return across_half(rows)

    plain = ((1,), (0,))

    def deliver(rows):
        blocks = send(rows)
        rows = jnp.concatenate(blocks, axis=0)
        return gather_parts(rows, "dp")

    rows_parts = deliver(dot(picks_now, both_tokens, plain))
    grad_parts = deliver(dot(picks_now, both_grads, plain) * gate_now)
    next_parts = deliver(dot(picks_next, both_grads, plain) * gate_next)

    order = lane ^ jnp.arange(ways, dtype=jnp.int32)
    weight_in = jnp.concatenate([w_in[0, 0], w_in[0, 1]], axis=1)
    weight_in = weight_in.reshape(ways, columns, 2 * hidden)
    weight_out = w_out[0].reshape(hidden, ways, columns)
    weight_in = [lax.dynamic_index_in_dim(weight_in, order[k], 0, False) for k in range(ways)]
    weight_out = [lax.dynamic_index_in_dim(weight_out, order[k], 1, False) for k in range(ways)]

    pre = sum(dot(rows_parts[k], weight_in[k], plain) for k in range(ways))
    gate_pre, up_value = pre[:, :hidden], pre[:, hidden:]
    sigmoid_gate = jax.nn.sigmoid(gate_pre)
    silu_gate = gate_pre * sigmoid_gate
    activation = (silu_gate * up_value).astype(jnp.bfloat16)
    activation, gate_pre, up_value = lax.optimization_barrier((activation, gate_pre, up_value))
    sigmoid_gate = jax.nn.sigmoid(gate_pre)
    silu_gate = gate_pre * sigmoid_gate
    held, mask, places = activation[None], half, [0]
    while mask > 1:
        held = jnp.concatenate([held, swap(held, "expert", mask)], axis=0)
        places += [k ^ mask for k in places]
        mask //= 2
    places = jnp.array(places, jnp.int32)

    def holder(target):
        wanted = source[target] ^ place
        return jnp.sum(jnp.where(places == wanted & -2, jnp.arange(half, dtype=jnp.int32), 0))

    other = swap(pick(held, holder(place ^ 1)), "expert", 1)
    shift = source[place] ^ place
    activation = jnp.where(shift & 1 == 1, other, pick(held, holder(place)))
    numbers = jnp.arange(devices, dtype=jnp.int32)
    numbers = 2 * ((numbers // 2) ^ (shift % half)) + (numbers & 1)
    activation = activation.reshape(devices, capacity, hidden)
    activation = pick(activation, numbers).reshape(slots, hidden)
    act_grad = sum(dot(grad_parts[k], weight_out[k], COLUMNS) for k in range(ways))
    gate_grad = act_grad * up_value * sigmoid_gate * (1.0 + gate_pre * (1.0 - sigmoid_gate))
    up_grad = act_grad * silu_gate
    both_grad = jnp.concatenate([gate_grad, up_grad], axis=1).astype(jnp.bfloat16)
    pieces = [dot(both_grad, w, COLUMNS).astype(jnp.bfloat16) for w in weight_in]
    summed = scatter_sum(pieces, "dp").astype(jnp.bfloat16)
    returned = jnp.concatenate(across_half(summed.reshape(half, 2 * capacity, columns)), axis=0)
    token_sums = dot(picks_now, returned, ((0,), (0,)))
    far_sums = cross(token_sums[tok_count:].astype(jnp.bfloat16))
    token_grad = (token_sums[:tok_count] + far_sums.astype(jnp.float32)).astype(jnp.bfloat16)

    weight_grad = jnp.stack([dot(activation, part, ROWS) for part in next_parts])
    begun = finish(0, lane, weight_grad, old_first, ())
    new_first, new_second, adam_step = finish(1, lane, weight_grad, old_second, begun)
    return (token_grad, new_first[None], new_second[None], adam_step[None])


def solution(mesh):
    return jax.shard_map(
        per_device,
        mesh=mesh,
        in_specs=(
            P("expert", "dp"),
            P("expert", "dp"),
            P("expert", None),
            P("expert", None),
            P(),
            P(),
            P("expert", None, None, "dp"),
            P("expert", "dp", None),
            P("expert", "dp", None),
            P("expert", "dp", None),
        ),
        out_specs=(
            P("expert", "dp"),
            P("expert", "dp", None),
            P("expert", "dp", None),
            P("expert", "dp", None),
        ),
        check_vma=False,
    )
```

```python
import jax
import jax.numpy as jnp
from jax import lax
from jax.experimental import pallas as pl
from jax.experimental.pallas import tpu as pltpu
from jax.sharding import PartitionSpec as P


beta_one = 0.9
beta_two = 0.95
epsilon = 1e-08


def swap(value, axis, mask):
    size = lax.axis_size(axis)
    return lax.ppermute(value, axis, [(j, j ^ mask) for j in range(size)])


def gather_parts(value, axis):
    parts = {0: value}
    mask = lax.axis_size(axis) // 2
    while mask:
        parts.update({k ^ mask: swap(v, axis, mask) for k, v in list(parts.items())})
        mask //= 2
    return [parts[k] for k in range(len(parts))]


def scatter_sum(parts, axis):
    parts = dict(enumerate(parts))
    mask = 1
    while len(parts) > 1:
        kept = {}
        for k in [k for k in parts if not k & mask]:
            other = swap(parts[k ^ mask].astype(jnp.bfloat16), axis, mask)
            kept[k] = parts[k].astype(jnp.float32) + other.astype(jnp.float32)
        parts = kept
        mask *= 2
    return parts[0]


def finish_body(lane_ref, grad_ref, first_ref, second_ref, *refs):
    out_first, out_second, out_step = refs[-3:]
    weight_grad = grad_ref[0]
    new_first = beta_one * first_ref[...].astype(jnp.float32) + (1.0 - beta_one) * weight_grad
    scaled = (1.0 - beta_two) * weight_grad * weight_grad
    new_second = beta_two * second_ref[...].astype(jnp.float32) + scaled
    out_first[...] = new_first
    out_second[...] = new_second
    out_step[...] = (new_first / (jnp.sqrt(new_second) + epsilon)).astype(jnp.bfloat16)


def finish(part, lane, weight_grad, moments, earlier):
    ways, hidden, columns = weight_grad.shape
    rows = max(hidden // 4, 16)
    few = ways // 2
    out = pl.BlockSpec((rows, columns), lambda d, i, lane: (i, part * few + d))
    kinds = (jnp.float32, jnp.float32, jnp.bfloat16)
    return pl.pallas_call(
        finish_body,
        out_shape=tuple(jax.ShapeDtypeStruct((hidden, ways * columns), kind) for kind in kinds),
        grid_spec=pltpu.PrefetchScalarGridSpec(
            num_scalar_prefetch=1,
            grid=(few, hidden // rows),
            in_specs=[
                pl.BlockSpec(
                    (1, rows, columns), lambda d, i, lane: (lane[0] ^ (part * few + d), i, 0)
                ),
                pl.BlockSpec((rows, columns), lambda d, i, lane: (i, d)),
                pl.BlockSpec((rows, columns), lambda d, i, lane: (i, few + d)),
            ]
            + [pl.BlockSpec(memory_space=pl.ANY)] * len(earlier),
            out_specs=(out, out, out),
        ),
        input_output_aliases={4 + k: k for k in range(len(earlier))},
    )(lane.reshape(1), weight_grad, moments, moments, *earlier)


def spread(value):
    return lax.all_to_all(value, "expert", split_axis=0, concat_axis=0, tiled=True)


def dot(left, right, dims):
    return lax.dot_general(left, right, (dims, ((), ())), preferred_element_type=jnp.float32)


ROWS = ((0,), (0,))
COLUMNS = ((1,), (1,))


def per_device(
    tokens,
    out_grad,
    routes,
    gate_weights,
    previous_home,
    next_home,
    w_in,
    w_out,
    first_moment,
    second_moment,
):
    devices = lax.axis_size("expert")
    ways = lax.axis_size("dp")
    half = devices // 2
    tok_count, top_count = routes.shape
    experts = previous_home.shape[0]
    capacity = tok_count * top_count * 9 // (8 * experts)
    slots = devices * capacity
    columns = tokens.shape[1]
    hidden = w_out.shape[1]
    place = lax.axis_index("expert")
    side = place // half
    lane = lax.axis_index("dp")

    homes = jnp.arange(devices, dtype=jnp.int32)
    matched = (next_home[:, None] == homes[None, :]).astype(jnp.int32)
    source = jnp.sum(matched * previous_home[:, None], axis=0)

    def pick(stack, index):
        return jnp.take(stack, index, axis=0, mode="clip")

    def relocate(value):
        rows = value.shape[0] // devices
        pieces = spread(value.reshape(devices, rows, value.shape[1]))
        pieces = pick(pieces, source)
        return spread(pieces).reshape(value.shape)

    def across_half(blocks):
        return [blocks[r] if r == 0 else swap(blocks[r], "expert", r) for r in range(half)]

    def cross(value):
        return swap(value, "expert", half)

    far_routes = cross(routes)
    far_gates = cross(gate_weights)
    far_tokens = cross(tokens)
    far_grads = cross(out_grad)

    middle = w_out.shape[2] // 2
    packed = []
    for cut in (slice(0, middle), slice(middle, None)):
        pieces = (first_moment[0][:, cut], second_moment[0][:, cut])
        packed.append(jnp.concatenate(pieces, axis=1).astype(jnp.bfloat16))
    old_first = relocate(packed[0])
    old_second = relocate(packed[1])

    both_routes = jnp.stack([routes, far_routes])
    both_gates = jnp.stack([gate_weights, far_gates])
    both_tokens = jnp.concatenate([tokens, far_tokens], axis=0)
    both_grads = jnp.concatenate([out_grad, far_grads], axis=0)
    block_side = jnp.stack([side, 1 - side]).astype(jnp.float32)
    earlier = jnp.tril(jnp.ones((tok_count, tok_count), jnp.bfloat16), -1)
    own_homes = place ^ jnp.arange(half, dtype=jnp.int32)

    def selection(home_table):
        chosen = (home_table[None, :] == own_homes[:, None]).astype(jnp.int32)
        expert_of = jnp.sum(chosen * jnp.arange(experts, dtype=jnp.int32)[None, :], axis=1)
        hit = both_routes[:, None, :, :] == expert_of[None, :, None, None]
        member = jnp.any(hit, axis=3)
        gate = jnp.sum(jnp.where(hit, both_gates[:, None, :, :], 0.0), axis=3)
        before = dot(member.astype(jnp.bfloat16), earlier, (((2,), (1,))))
        slot = jnp.where(member, before + block_side[:, None, None] * capacity, -1.0)
        slot = jnp.concatenate([slot[0], slot[1]], axis=1)
        gate = jnp.concatenate([gate[0], gate[1]], axis=1)
        numbers = lax.broadcasted_iota(jnp.int32, (half, 2 * capacity, 2 * tok_count), 1)
        picks = numbers == slot.astype(jnp.int32)[:, None, :]
        slot_gate = jnp.sum(jnp.where(picks, gate[:, None, :], 0.0), axis=2)
        picks = picks.astype(jnp.bfloat16).reshape(slots, 2 * tok_count)
        return picks, slot_gate.reshape(slots, 1)

    picks_now, gate_now = selection(previous_home)
    picks_next, gate_next = selection(next_home)

    def send(rows):
        rows = rows.astype(jnp.bfloat16).reshape(half, 2 * capacity, columns)
        return across_half(rows)

    plain = ((1,), (0,))

    def deliver(rows):
        blocks = send(rows)
        rows = jnp.concatenate(blocks, axis=0)
        return gather_parts(rows, "dp")

    rows_parts = deliver(dot(picks_now, both_tokens, plain))
    grad_parts = deliver(dot(picks_now, both_grads, plain) * gate_now)
    next_parts = deliver(dot(picks_next, both_grads, plain) * gate_next)

    order = lane ^ jnp.arange(ways, dtype=jnp.int32)
    weight_in = jnp.concatenate([w_in[0, 0], w_in[0, 1]], axis=1)
    weight_in = weight_in.reshape(ways, columns, 2 * hidden)
    weight_in = [lax.dynamic_index_in_dim(weight_in, order[k], 0, False) for k in range(ways)]
    weight_out = [
        lax.dynamic_slice(w_out[0], (0, order[k] * columns), (hidden, columns))
        for k in range(ways)
    ]

    pre = sum(dot(rows_parts[k], weight_in[k], plain) for k in range(ways))
    gate_pre, up_value = pre[:, :hidden], pre[:, hidden:]
    sigmoid_gate = jax.nn.sigmoid(gate_pre)
    silu_gate = gate_pre * sigmoid_gate
    activation = (silu_gate * up_value).astype(jnp.bfloat16)
    activation, gate_pre, up_value = lax.optimization_barrier((activation, gate_pre, up_value))
    sigmoid_gate = jax.nn.sigmoid(gate_pre)
    silu_gate = gate_pre * sigmoid_gate
    held, mask, places = activation[None], half, [0]
    while mask > 1:
        held = jnp.concatenate([held, swap(held, "expert", mask)], axis=0)
        places += [k ^ mask for k in places]
        mask //= 2
    places = jnp.array(places, jnp.int32)

    def holder(target):
        wanted = source[target] ^ place
        return jnp.sum(jnp.where(places == wanted & -2, jnp.arange(half, dtype=jnp.int32), 0))

    other = swap(pick(held, holder(place ^ 1)), "expert", 1)
    shift = source[place] ^ place
    activation = jnp.where(shift & 1 == 1, other, pick(held, holder(place)))
    numbers = jnp.arange(devices, dtype=jnp.int32)
    numbers = 2 * ((numbers // 2) ^ (shift % half)) + (numbers & 1)
    activation = activation.reshape(devices, capacity, hidden)
    activation = pick(activation, numbers).reshape(slots, hidden)
    act_grad = sum(dot(grad_parts[k], weight_out[k], COLUMNS) for k in range(ways))
    gate_grad = act_grad * up_value * sigmoid_gate * (1.0 + gate_pre * (1.0 - sigmoid_gate))
    up_grad = act_grad * silu_gate
    both_grad = jnp.concatenate([gate_grad, up_grad], axis=1).astype(jnp.bfloat16)
    pieces = [dot(both_grad, w, COLUMNS).astype(jnp.bfloat16) for w in weight_in]
    summed = scatter_sum(pieces, "dp").astype(jnp.bfloat16)
    returned = jnp.concatenate(across_half(summed.reshape(half, 2 * capacity, columns)), axis=0)
    token_sums = dot(picks_now, returned, ((0,), (0,)))
    far_sums = cross(token_sums[tok_count:].astype(jnp.bfloat16))
    token_grad = (token_sums[:tok_count] + far_sums.astype(jnp.float32)).astype(jnp.bfloat16)

    weight_grad = jnp.stack([dot(activation, part, ROWS) for part in next_parts])
    begun = finish(0, lane, weight_grad, old_first, ())
    new_first, new_second, adam_step = finish(1, lane, weight_grad, old_second, begun)
    return (token_grad, new_first[None], new_second[None], adam_step[None])


def solution(mesh):
    return jax.shard_map(
        per_device,
        mesh=mesh,
        in_specs=(
            P("expert", "dp"),
            P("expert", "dp"),
            P("expert", None),
            P("expert", None),
            P(),
            P(),
            P("expert", None, None, "dp"),
            P("expert", "dp", None),
            P("expert", "dp", None),
            P("expert", "dp", None),
        ),
        out_specs=(
            P("expert", "dp"),
            P("expert", "dp", None),
            P("expert", "dp", None),
            P("expert", "dp", None),
        ),
        check_vma=False,
    )
```
